512 devices in a mesh: ia: 16 (over y, z_hi), ja: 32 (over x, z_lo, core).
Axes of the slice: x: 4, y: 4, z: 16 (z_hi: 4, z_lo: 4; z = z_hi * 4 + z_lo), core: 2. Of those that a mesh axis runs over, the one named last changes fastest.
Arguments:
- amplitudes: float32 [16, 32, 512, 512], P('ia', 'ja'), may hold values from -3 to 3
- integrals: bfloat16 [16, 32, 512, 512], P('ia', 'ja'), may hold values from -6 to 6
- pao_fock: float32 [8, 64, 384], replicated, may hold values from -0.3125 to 0.3125
- pao_intersection: float32 [8, 64, 384], replicated, may hold values from -1 to 2
- block_columns: int32 [8, 6], replicated, may hold values from 0 to 7, as said below
- occ_fock: float32 [32, 32], replicated, may hold values from -1 to 0.8, as said below
- pao_energies: float32 [512], replicated, may hold values from 0.3 to 2
- row_links: int32 [16, 32, 4], P('ia', 'ja'), may hold values 0 or 1
- column_links: int32 [16, 32, 2], P('ia', 'ja'), may hold values 0 or 1
Outputs:
- updated: float32 [16, 32, 512, 512], P('ia', 'ja')
The draws below stay inside these ranges and needn't reach their ends.
Inputs may be any that keep to these rules, and one draw needn't show every extreme that they name: `block_columns`: slot 0 of block row r holds r; the slots of a row hold distinct block columns. `occ_fock`: Symmetric; its diagonal lies between -1 and -0.3.
All inputs are finite; a program needn't handle non-finite values. No bound on the sum of `row_links` or of `column_links` on one device may be relied on, other than what follows from the above.
Results may differ from the reference program's by a relative error of at most 0.0003.
Values sent between devices are 32-bit elements; how exact they have to be, the bound alone decides.
No kernel may reach another device: no remote copies, remote signals or barrier semaphores. Data moves between devices by JAX's collectives and lax.ppermute only.
A program may use at most 64 MiB of HBM per device.

```python
import math
import jax
import jax.numpy as jnp
from jax import lax

P_SIZE = 512
BLK = 64
NZ = 6
ITERS = 2
NB = 8
NI = 16
NJ = 32


def draw_block_columns(key, part):
    scores = jax.random.randint(key, (NB, NB), 0, 1 << 20) * NB + jnp.arange(NB, dtype=jnp.int32)[None, :]
    scores = jnp.where(jnp.eye(NB, dtype=bool), -1, scores)
    order = jnp.argsort(scores, axis=1)
    return order[:, :NZ].astype(jnp.int32)


def draw_pao_intersection(key, part):
    spread = (NZ * BLK) ** (-0.5)
    noise = jax.random.truncated_normal(key, -4.0, 4.0, (NB, BLK, NZ * BLK), jnp.float32) * spread
    identity = jnp.concatenate([jnp.eye(BLK, dtype=jnp.float32), jnp.zeros((BLK, (NZ - 1) * BLK), jnp.float32)], axis=1)
    return noise + identity[None, :, :]


def draw_occ_fock(key, part):
    key_off = jax.random.fold_in(key, 11)
    key_diag = jax.random.fold_in(key, 12)
    raw = jax.random.uniform(key_off, (NJ, NJ), jnp.float32, -0.8, 0.8)
    diagonal_part = jax.random.uniform(key_diag, (NJ,), jnp.float32, 0.3, 1.0)
    upper = jnp.triu(raw, 1)
    return upper + upper.T - jnp.diag(diagonal_part)


def plant(array, rng, least, high):
    longest = array.shape.index(max(array.shape))
    spots = []
    for shift in (0, 1):
        where = [jax.random.randint(jax.random.fold_in(rng, axis), (), 0, length) for axis, length in enumerate(array.shape)]
        where[longest] = (where[longest] + shift) % array.shape[longest]
        spots.append(tuple(where))
    return array.at[spots[0]].set(least).at[spots[1]].set(high)


def steps_of(key, dims, shards, low, top_value):
    gain = 1.0
    for dim, blocks in shards:
        steps = jax.random.uniform(jax.random.fold_in(jax.random.fold_in(key, 6), dim), (blocks,), jnp.float32, low / len(shards), top_value / len(shards))
        gain = gain * jnp.repeat(jnp.exp(steps), dims[dim] // blocks).reshape((-1,) + (1,) * (len(dims) - 1 - dim))
    return gain


def centred(stream_key, shape, scale, reach, cuts=(), kind=jnp.bfloat16):
    drawn = scale * jax.random.normal(stream_key, shape, jnp.float32)
    if cuts:
        drawn = drawn * steps_of(stream_key, shape, cuts, -0.22, 0.18)
    return jnp.clip(drawn, -reach, reach).astype(kind)


def setup_inputs(seed: int = 0) -> dict:
    streams_of = jax.random.split(jax.random.key(seed), 10)
    return {
        "amplitudes": centred(streams_of[0], (NI, NJ, P_SIZE, P_SIZE), 0.5, 3.0, ((0, 16), (1, 32)), jnp.float32),
        "integrals": centred(streams_of[1], (NI, NJ, P_SIZE, P_SIZE), 1.0, 6.0, ((0, 16), (1, 32))),
        "pao_fock": centred(streams_of[2], (NB, BLK, NZ * BLK), (NZ * BLK) ** -0.5, 0.3125, (), jnp.float32),
        "pao_intersection": draw_pao_intersection(jax.random.fold_in(streams_of[9], 71), 0),
        "block_columns": draw_block_columns(jax.random.fold_in(streams_of[9], 71), 0),
        "occ_fock": draw_occ_fock(jax.random.fold_in(streams_of[9], 71), 0),
        "pao_energies": jnp.clip(jnp.exp(jax.random.uniform(streams_of[6], (P_SIZE,), jnp.float32, math.log(0.3), math.log(2.0))), 0.3, 2.0),
        "row_links": plant((jax.random.randint(streams_of[7], (NI, NJ, 4), 0, 2) < 1).astype(jnp.int32), jax.random.fold_in(streams_of[7], 1), 0, 1),
        "column_links": plant((jax.random.randint(streams_of[8], (NI, NJ, 2), 0, 2) < 1).astype(jnp.int32), jax.random.fold_in(streams_of[8], 1), 0, 1),
    }


HIGH = lax.Precision.HIGHEST


def build_dense(blocks, columns):
    block_rows, block_size, block_wide = blocks.shape
    stored = block_wide // block_size
    onehot = (columns[:, :, None] == jnp.arange(block_rows, dtype=jnp.int32)[None, None, :]).astype(jnp.float32)
    split_blocks = blocks.reshape(block_rows, block_size, stored, block_size)
    dense = jnp.einsum("rxcb,rcn->rxnb", split_blocks, onehot, precision=HIGH)
    return dense.reshape(block_rows * block_size, block_rows * block_size)


def pair_residual(fock_dense, intersection_dense, amps_pair, coupled, integral):
    fock_left = jnp.dot(fock_dense, amps_pair, precision=HIGH)
    intersection_coupled = jnp.dot(intersection_dense, coupled, precision=HIGH)
    intersection_amps = jnp.dot(intersection_dense, amps_pair, precision=HIGH)
    first_term = jnp.dot(fock_left - intersection_coupled, intersection_dense, precision=HIGH)
    second_term = jnp.dot(intersection_amps, fock_dense, precision=HIGH)
    return integral.astype(jnp.float32) + first_term + second_term


def displaced(stack, axis_number, offset):
    length = stack.shape[axis_number]
    widths = [(0, 0)] * stack.ndim
    widths[axis_number] = (max(-offset, 0), max(offset, 0))
    padded = jnp.pad(stack, widths)
    return lax.slice_in_dim(padded, max(offset, 0), max(offset, 0) + length, axis=axis_number)


def reference(amplitudes, integrals, pao_fock, pao_intersection, block_columns, occ_fock, pao_energies, row_links, column_links):
    fock_dense = build_dense(pao_fock, block_columns)
    intersection_dense = build_dense(pao_intersection, block_columns)
    first_ids = jnp.arange(NI, dtype=jnp.int32)[:, None] + jnp.zeros((1, NJ), jnp.int32)
    second_ids = jnp.zeros((NI, 1), jnp.int32) + jnp.arange(NJ, dtype=jnp.int32)[None, :]
    diagonal_occ = jnp.diagonal(occ_fock)
    diag_sum = diagonal_occ[:NI][:, None] + diagonal_occ[None, :]
    energy_sum = pao_energies[:, None] + pao_energies[None, :]
    batched = jax.vmap(pair_residual, in_axes=(None, None, 0, 0, 0))

    def update_row(packed):
        row_amps, row_coupled, row_integrals, diag_first = packed
        energy_gap = energy_sum[None, :, :] - diag_first - diagonal_occ[:, None, None]
        residual = batched(fock_dense, intersection_dense, row_amps, row_coupled, row_integrals)
        return row_amps - residual * (1.0 / energy_gap)

    current = amplitudes
    for sweep_number in range(ITERS):
        coupled = diag_sum[:, :, None, None] * current
        for slot_number, offset in enumerate((-1, 1)):
            target = first_ids + offset
            inside = ((target >= 0) & (target < NI)).astype(jnp.float32)
            coefficient = occ_fock[first_ids, jnp.clip(target, 0, NJ - 1)] * inside * column_links[:, :, slot_number].astype(jnp.float32)
            coupled = coupled + coefficient[:, :, None, None] * displaced(current, 0, offset)
        for slot_number, offset in enumerate((-2, -1, 1, 2)):
            target = second_ids + offset
            inside = ((target >= 0) & (target < NJ)).astype(jnp.float32)
            coefficient = occ_fock[jnp.clip(target, 0, NJ - 1), second_ids] * inside * row_links[:, :, slot_number].astype(jnp.float32)
            coupled = coupled + coefficient[:, :, None, None] * displaced(current, 1, offset)
        current = lax.map(update_row, (current, coupled, integrals, diagonal_occ[:NI]))
    return current
```

```python
import jax
import jax.numpy as jnp
from jax import lax
from jax.sharding import PartitionSpec as P

ITERS = 2
CHUNKS = 2
NX, NY, NHI, NLO = 4, 4, 4, 4
NZ = NHI * NLO
NI = NY * NHI
NJ = NX * NLO * 2

HIGH = lax.Precision.HIGH
AXES = ("ia", "ja")


def chip(i, j):
    return j // (2 * NLO), i // NHI, (i % NHI) * NLO + (j // 2) % NLO, j % 2


def pair(x, y, z, c):
    z = z % NZ
    return y * NHI + z // NLO, (x * NLO + z % NLO) * 2 + c


def moves(target):
    pairs = []
    for i in range(NI):
        for j in range(NJ):
            to = target(i, j)
            if to is not None:
                pairs.append((i * NJ + j, to[0] * NJ + to[1]))
    return pairs


def first_leg(step):
    def target(i, j):
        if not 0 <= i + step < NI:
            return None
        x, y, z, c = chip(i, j)
        return pair(x, (i + step) // NHI, z + step, c)

    return moves(target)


def middle_leg(step):
    def target(i, j):
        x, y, z, c = chip(i, j)
        di, dj = pair(x, y, z + 3 * step, c)
        edge = NLO - 1 if step > 0 else 0
        if not 0 <= di - step < NI and (dj // 2) % NLO != edge:
            return None
        return pair(x, y, z + 2 * step, c)

    return moves(target)


def last_leg(step):
    def target(i, j):
        x, y, z, c = chip(i, j)
        di, dj = pair(x, y, z + step, c)
        near = 0 if step > 0 else NLO - 1
        if not 0 <= di - step < NI and (dj // 2) % NLO == near:
            return None
        return di, dj

    return moves(target)


def across(i, j):
    x, y, z, c = chip(i, j)
    if z % NLO == NLO - 1 and x + 1 < NX:
        return pair(x + 1, y, z, c)
    if z % NLO == 0 and x > 0:
        return pair(x - 1, y, z, c)
    return None


def goal_links(step):
    def target(i, j):
        x, y, z, c = chip(i, j)
        return pair(x, y, z - 3 * step, c)

    return moves(target)


def along_j(offset):
    def target(i, j):
        return (i, j + offset) if 0 <= j + offset < NJ else None

    return moves(target)


FIRST = {s: first_leg(s) for s in (1, -1)}
MIDDLE = {s: middle_leg(s) for s in (1, -1)}
LAST = {s: last_leg(s) for s in (1, -1)}
ACROSS = moves(across)
PARTNER = moves(lambda i, j: (i, j ^ 1))
GOAL = {s: goal_links(s) for s in (1, -1)}


def send(x, pairs):
    return lax.ppermute(x, AXES, pairs)


def mm(a, b):
    return jnp.dot(a, b, precision=HIGH, preferred_element_type=jnp.float32)


def build_dense(blocks, columns):
    block_rows, block_size, block_wide = blocks.shape
    stored = block_wide // block_size
    onehot = (columns[:, :, None] == jnp.arange(block_rows, dtype=jnp.int32)[None, None, :]).astype(
        jnp.float32
    )
    split_blocks = blocks.reshape(block_rows, block_size, stored, block_size)
    dense = jnp.einsum("rxcb,rcn->rxnb", split_blocks, onehot, precision=lax.Precision.HIGHEST)
    return dense.reshape(block_rows * block_size, block_rows * block_size)


def coefficients(occ_fock, row_links, column_links):
    i = lax.axis_index("ia").astype(jnp.int32)
    j = lax.axis_index("ja").astype(jnp.int32)
    core = j % 2
    low = (j // 2) % NLO
    z = (i % NHI) * NLO + low
    up = (i // NHI) * NHI + ((z + 3) % NZ) // NLO
    down = (i // NHI) * NHI + ((z + NZ - 3) % NZ) // NLO
    mate = j + 1 - 2 * core
    far = send(row_links, along_j(-2))
    back = send(row_links, along_j(2))
    ahead = send(column_links, GOAL[1])
    behind = send(column_links, GOAL[-1])
    none = jnp.int32(-1)
    rows = jnp.stack([up, down, j, j + 1, j, j - 1, mate, i, j])
    columns = jnp.stack(
        [up - 1, jnp.where(down + 1 < NI, down + 1, none), j + 2, j + 2, j - 2, j - 2, j, i, j]
    )
    one = jnp.int32(1)
    weights = jnp.stack(
        [
            ahead[0],
            behind[1],
            far[0],
            far[1] * (1 - core),
            back[3],
            back[2] * core,
            jnp.where(core == 0, row_links[2], row_links[1]),
            one,
            one,
        ]
    ).astype(jnp.float32)
    places = jnp.arange(NJ, dtype=jnp.int32)
    hot = (rows[:, None, None] == places[None, :, None]) & (columns[:, None, None] == places[None, None, :])
    picked = jnp.sum(jnp.where(hot, occ_fock[None], 0.0), axis=(1, 2)) * weights
    return picked, low


def sweep_pieces(current, picked, low):
    wide = current.shape[0] // CHUNKS
    at_top = (low == NLO - 1).astype(jnp.float32)
    at_bottom = (low == 0).astype(jnp.float32)
    own_up, mate_up, own_down, mate_down = picked[2], picked[3], picked[4], picked[5]
    pieces = [current[k * wide : (k + 1) * wide] for k in range(CHUNKS)]
    mates = [send(p, PARTNER) for p in pieces]
    firsts = [{s: send(p, FIRST[s]) for s in (1, -1)} for p in pieces]
    crossed = []
    for p, m in zip(pieces, mates):
        out = (at_top * own_up + at_bottom * own_down) * p + (at_top * mate_up + at_bottom * mate_down) * m
        crossed.append(send(out, ACROSS))
    middles = []
    for f, x in zip(firsts, crossed):
        middles.append(
            {
                1: send(picked[0] * f[1] + at_bottom * x, MIDDLE[1]),
                -1: send(picked[1] * f[-1] + at_top * x, MIDDLE[-1]),
            }
        )
    gathered = []
    for p, m, mid in zip(pieces, mates, middles):
        keep_up = 1.0 - at_top
        keep_down = 1.0 - at_bottom
        plus = send(mid[1] + (keep_up * own_up) * p + (keep_up * mate_up) * m, LAST[1])
        minus = send(mid[-1] + (keep_down * own_down) * p + (keep_down * mate_down) * m, LAST[-1])
        gathered.append(plus + minus + picked[6] * m)
    return gathered


def body(
    amplitudes,
    integrals,
    pao_fock,
    pao_intersection,
    block_columns,
    occ_fock,
    pao_energies,
    row_links,
    column_links,
):
    current = amplitudes[0, 0]
    integral = integrals[0, 0]
    picked, low = coefficients(occ_fock, row_links[0, 0], column_links[0, 0])
    diagonal = picked[7] + picked[8]
    fock_dense = build_dense(pao_fock, block_columns)
    intersection_dense = build_dense(pao_intersection, block_columns)
    shifted = fock_dense - diagonal * intersection_dense
    inverse_gap = 1.0 / (pao_energies[:, None] + pao_energies[None, :] - diagonal)
    wide = current.shape[0] // CHUNKS
    for sweep_number in range(ITERS):
        gathered = sweep_pieces(current, picked, low)
        local = mm(mm(shifted, current), intersection_dense) + mm(mm(intersection_dense, current), fock_dense)
        local = local + integral.astype(jnp.float32)
        for k, piece in enumerate(gathered):
            left = intersection_dense[:, k * wide : (k + 1) * wide]
            local = local - mm(left, mm(piece, intersection_dense))
        current = current - local * inverse_gap
    return current[None, None]


def solution(mesh):
    placed = (
        P("ia", "ja", None, None),
        P("ia", "ja", None, None),
        P(),
        P(),
        P(),
        P(),
        P(),
        P("ia", "ja", None),
        P("ia", "ja", None),
    )
    return jax.shard_map(
        body, mesh=mesh, in_specs=placed, out_specs=P("ia", "ja", None, None), check_vma=False
    )
```

```python
import jax
import jax.numpy as jnp
import numpy as np
from jax import lax
from jax.sharding import PartitionSpec as P

ITERS = 2
CHUNKS = 2
NX, NY, NHI, NLO = 4, 4, 4, 4
NZ = NHI * NLO
NI = NY * NHI
NJ = NX * NLO * 2

HIGH = lax.Precision.HIGH
AXES = ("ia", "ja")


def chip(i, j):
    return j // (2 * NLO), i // NHI, (i % NHI) * NLO + (j // 2) % NLO, j % 2


def pair(x, y, z, c):
    z = z % NZ
    return y * NHI + z // NLO, (x * NLO + z % NLO) * 2 + c


def moves(target):
    pairs = []
    for i in range(NI):
        for j in range(NJ):
            to = target(i, j)
            if to is not None:
                pairs.append((i * NJ + j, to[0] * NJ + to[1]))
    return pairs


def first_leg(step):
    def target(i, j):
        if not 0 <= i + step < NI:
            return None
        x, _, z, c = chip(i, j)
        return pair(x, (i + step) // NHI, z + step, c)

    return moves(target)


def middle_leg(step):
    def target(i, j):
        x, y, z, c = chip(i, j)
        di, dj = pair(x, y, z + 3 * step, c)
        edge = NLO - 1 if step > 0 else 0
        if not 0 <= di - step < NI and (dj // 2) % NLO != edge:
            return None
        return pair(x, y, z + 2 * step, c)

    return moves(target)


def last_leg(step):
    def target(i, j):
        x, y, z, c = chip(i, j)
        di, dj = pair(x, y, z + step, c)
        near = 0 if step > 0 else NLO - 1
        if not 0 <= di - step < NI and (dj // 2) % NLO == near:
            return None
        return di, dj

    return moves(target)


def across(i, j):
    x, y, z, c = chip(i, j)
    if z % NLO == NLO - 1 and x + 1 < NX:
        return pair(x + 1, y, z, c)
    if z % NLO == 0 and x > 0:
        return pair(x - 1, y, z, c)
    return None


def goal_links(step):
    def target(i, j):
        x, y, z, c = chip(i, j)
        return pair(x, y, z - 3 * step, c)

    return moves(target)


def along_j(offset):
    def target(i, j):
        return (i, j + offset) if 0 <= j + offset < NJ else None

    return moves(target)


FIRST = {s: first_leg(s) for s in (1, -1)}
MIDDLE = {s: middle_leg(s) for s in (1, -1)}
LAST = {s: last_leg(s) for s in (1, -1)}
ACROSS = moves(across)
PARTNER = moves(lambda i, j: (i, j ^ 1))
GOAL = {s: goal_links(s) for s in (1, -1)}


def send(x, pairs):
    return lax.ppermute(x, AXES, pairs)


def mm(a, b):
    return jnp.dot(a, b, precision=HIGH, preferred_element_type=jnp.float32)


def build_dense(blocks, columns):
    block_rows, block_size, block_wide = blocks.shape
    wide = block_rows * block_size
    slot = jnp.arange(block_wide, dtype=jnp.int32)
    place = jnp.repeat(columns, block_size, axis=1) * block_size + (slot % block_size)[None, :]
    spread = (place[:, :, None] == jnp.arange(wide, dtype=jnp.int32)[None, None, :]).astype(jnp.float32)
    dense = jnp.einsum("rxk,rkn->rxn", blocks, spread, precision=HIGH)
    return dense.reshape(wide, wide)


SOURCES = ("own", "far", "back", "ahead", "behind")
ROW, COLUMN = 0, 4
LINKS = (
    ("ahead", COLUMN),
    ("behind", COLUMN + 1),
    ("far", ROW),
    ("far", ROW + 1),
    ("back", ROW + 3),
    ("back", ROW + 2),
    ("far", ROW),
    ("far", ROW + 1),
    ("back", ROW + 3),
    ("back", ROW + 2),
    ("own", ROW + 2),
    ("own", ROW + 1),
    None,
    None,
)


def tables():
    places = np.zeros((NI, NJ, len(LINKS), 3), np.int32)
    for i in range(NI):
        for j in range(NJ):
            x, y, z, c = chip(i, j)
            low = z % NLO
            up = pair(x, y, z + 3, c)[0]
            down = pair(x, y, z - 3, c)[0]
            top, bottom = low == NLO - 1, low == 0
            odd, even = c == 1, c == 0
            places[i, j] = [
                (up, up - 1, up > 0),
                (down, down + 1, down + 1 < NI),
                (j, j + 2, not top),
                (j + 1, j + 2, even and not top),
                (j, j - 2, not bottom),
                (j - 1, j - 2, odd and not bottom),
                (j, j + 2, top),
                (j + 1, j + 2, even and top),
                (j, j - 2, bottom),
                (j - 1, j - 2, odd and bottom),
                (j + 1, j, even),
                (j - 1, j, odd),
                (i, i, True),
                (j, j, True),
            ]
    return places.reshape(NI * NJ, len(LINKS), 3)


TABLE = tables()
CHOICE = np.zeros((len(LINKS), len(SOURCES) * 8), np.float32)
for entry, link in enumerate(LINKS):
    if link is not None:
        CHOICE[entry, SOURCES.index(link[0]) * 8 + link[1]] = 1.0
FREE = np.array([1.0 if link is None else 0.0 for link in LINKS], np.float32)


def coefficients(occ_fock, row_links, column_links):
    links = jnp.concatenate([row_links, column_links, jnp.zeros((2,), jnp.int32)])
    got = {
        "own": links,
        "far": send(links, along_j(-2)),
        "back": send(links, along_j(2)),
        "ahead": send(links, GOAL[1]),
        "behind": send(links, GOAL[-1]),
    }
    flat = jnp.concatenate([got[name] for name in SOURCES]).astype(jnp.float32)
    where = lax.axis_index("ia") * NJ + lax.axis_index("ja")
    place = lax.dynamic_slice_in_dim(jnp.asarray(TABLE), where, 1, axis=0)[0]
    rows, columns, used = place[:, 0], place[:, 1], place[:, 2]
    spots = jnp.arange(NJ, dtype=jnp.int32)
    hot = (rows[:, None, None] == spots[None, :, None]) & (columns[:, None, None] == spots[None, None, :])
    picked = jnp.sum(jnp.where(hot, occ_fock[None], 0.0), axis=(1, 2))
    weights = jnp.sum(jnp.asarray(CHOICE) * flat[None, :], axis=1) + jnp.asarray(FREE)
    return picked * weights * used.astype(jnp.float32)


def after(values, earlier):
    kept = lax.optimization_barrier((*values, earlier))
    return kept[: len(values)]


def sweep_pieces(pieces, picked, low):
    at_top = (low == NLO - 1).astype(jnp.float32)
    at_bottom = (low == 0).astype(jnp.float32)
    mates = [send(p, PARTNER) for p in pieces]
    firsts = [{s: send(p, FIRST[s]) for s in (1, -1)} for p in pieces]
    crossed = []
    out = None
    for p, m in zip(pieces, mates):
        if out is not None:
            (m,) = after((m,), out)
        out = (picked[6] + picked[8]) * p + (picked[7] + picked[9]) * m
        crossed.append(send(out, ACROSS))
    middles = []
    up = None
    for f, x in zip(firsts, crossed):
        if up is not None:
            (x,) = after((x,), up)
        up = picked[0] * f[1] + at_bottom * x
        down = picked[1] * f[-1] + at_top * x
        middles.append({1: send(up, MIDDLE[1]), -1: send(down, MIDDLE[-1])})
    gathered = []
    up = None
    for p, m, mid in zip(pieces, mates, middles):
        if up is not None:
            p, m = after((p, m), up)
        up = mid[1] + picked[2] * p + picked[3] * m
        down = mid[-1] + picked[4] * p + picked[5] * m
        plus = send(up, LAST[1])
        minus = send(down, LAST[-1])
        gathered.append(plus + minus + (picked[10] + picked[11]) * m)
    return gathered


def body(
    amplitudes,
    integrals,
    pao_fock,
    pao_intersection,
    block_columns,
    occ_fock,
    pao_energies,
    row_links,
    column_links,
):
    start = amplitudes[0, 0]
    integral = integrals[0, 0]
    low = (lax.axis_index("ja") // 2) % NLO
    wide = start.shape[0] // CHUNKS
    spans = [slice(k * wide, (k + 1) * wide) for k in range(CHUNKS)]
    pieces = list(lax.optimization_barrier(tuple(start[span] for span in spans)))
    for sweep_number in range(ITERS):
        if sweep_number == 0:
            picked = coefficients(occ_fock, row_links[0, 0], column_links[0, 0])
            diagonal = picked[12] + picked[13]
            fock_dense = build_dense(pao_fock, block_columns)
            intersection_dense = build_dense(pao_intersection, block_columns)
            shifted = fock_dense - diagonal * intersection_dense
            inverse_gap = 1.0 / (pao_energies[:, None] + pao_energies[None, :] - diagonal)
            current = start
        else:
            current = jnp.concatenate(pieces, axis=0)
        gathered = sweep_pieces(pieces, picked, low)
        local = mm(mm(shifted, current), intersection_dense)
        local = local + mm(mm(intersection_dense, current), fock_dense)
        local = local + integral.astype(jnp.float32)
        rights = [mm(coupled, intersection_dense) for coupled in gathered]
        if sweep_number + 1 == ITERS:
            for right, span in zip(rights, spans):
                local = local - mm(intersection_dense[:, span], right)
            return (current - local * inverse_gap)[None, None]
        rest = [local[span] for span in spans]
        for k, right in enumerate(rights):
            rest = [r - mm(intersection_dense[span, spans[k]], right) for r, span in zip(rest, spans)]
        pieces = [p - r * inverse_gap[span] for p, r, span in zip(pieces, rest, spans)]


def solution(mesh):
    placed = (
        P("ia", "ja", None, None),
        P("ia", "ja", None, None),
        P(),
        P(),
        P(),
        P(),
        P(),
        P("ia", "ja", None),
        P("ia", "ja", None),
    )
    return jax.shard_map(
        body, mesh=mesh, in_specs=placed, out_specs=P("ia", "ja", None, None), check_vma=False
    )
```

```python
import jax
import jax.numpy as jnp
import numpy as np
from jax import lax
from jax.sharding import PartitionSpec as P

ITERS = 2
CHUNKS = 2
NX, NY, NHI, NLO = 4, 4, 4, 4
NZ = NHI * NLO
NI = NY * NHI
NJ = NX * NLO * 2

HIGH = lax.Precision.HIGH
AXES = ("ia", "ja")


def chip(i, j):
    return j // (2 * NLO), i // NHI, (i % NHI) * NLO + (j // 2) % NLO, j % 2


def pair(x, y, z, c):
    z = z % NZ
    return y * NHI + z // NLO, (x * NLO + z % NLO) * 2 + c


def moves(target):
    pairs = []
    for i in range(NI):
        for j in range(NJ):
            to = target(i, j)
            if to is not None:
                pairs.append((i * NJ + j, to[0] * NJ + to[1]))
    return pairs


def first_leg(step):
    def target(i, j):
        if not 0 <= i + step < NI:
            return None
        x, _, z, c = chip(i, j)
        return pair(x, (i + step) // NHI, z + step, c)

    return moves(target)


def middle_leg(step):
    def target(i, j):
        x, y, z, c = chip(i, j)
        di, dj = pair(x, y, z + 3 * step, c)
        edge = NLO - 1 if step > 0 else 0
        if not 0 <= di - step < NI and (dj // 2) % NLO != edge:
            return None
        return pair(x, y, z + 2 * step, c)

    return moves(target)


def last_leg(step):
    def target(i, j):
        x, y, z, c = chip(i, j)
        di, dj = pair(x, y, z + step, c)
        near = 0 if step > 0 else NLO - 1
        if not 0 <= di - step < NI and (dj // 2) % NLO == near:
            return None
        return di, dj

    return moves(target)


def across(i, j):
    x, y, z, c = chip(i, j)
    if z % NLO == NLO - 1 and x + 1 < NX:
        return pair(x + 1, y, z, c)
    if z % NLO == 0 and x > 0:
        return pair(x - 1, y, z, c)
    return None


def goal_links(step):
    def target(i, j):
        x, y, z, c = chip(i, j)
        return pair(x, y, z - 3 * step, c)

    return moves(target)


def along_j(offset):
    def target(i, j):
        return (i, j + offset) if 0 <= j + offset < NJ else None

    return moves(target)


FIRST = {s: first_leg(s) for s in (1, -1)}
MIDDLE = {s: middle_leg(s) for s in (1, -1)}
LAST = {s: last_leg(s) for s in (1, -1)}
ACROSS = moves(across)
PARTNER = moves(lambda i, j: (i, j ^ 1))
GOAL = {s: goal_links(s) for s in (1, -1)}


def send(x, pairs):
    return lax.ppermute(x, AXES, pairs)


def mm(a, b):
    return jnp.dot(a, b, precision=HIGH, preferred_element_type=jnp.float32)


def build_dense(blocks, columns):
    block_rows, block_size, block_wide = blocks.shape
    wide = block_rows * block_size
    slot = jnp.arange(block_wide, dtype=jnp.int32)
    place = jnp.repeat(columns, block_size, axis=1) * block_size + (slot % block_size)[None, :]
    spread = (place[:, :, None] == jnp.arange(wide, dtype=jnp.int32)[None, None, :]).astype(jnp.float32)
    dense = jnp.einsum("rxk,rkn->rxn", blocks, spread, precision=HIGH)
    return dense.reshape(wide, wide)


SOURCES = ("own", "far", "back", "ahead", "behind")
LINK = {name: 8 * n for n, name in enumerate(SOURCES)}
UNIT = 8 * len(SOURCES)
AHEAD, BEHIND, UP, UP_MATE, DOWN, DOWN_MATE, OUT, OUT_MATE, MATE, FIRST_DIAGONAL, SECOND_DIAGONAL = range(11)
COLUMN = 4


def tables():
    places = np.zeros((NI * NJ, 11, 4), np.int32)
    for i in range(NI):
        for j in range(NJ):
            x, y, z, c = chip(i, j)
            low = z % NLO
            up = pair(x, y, z + 3, c)[0]
            down = pair(x, y, z - 3, c)[0]
            top, bottom = low == NLO - 1, low == 0
            odd, even = c == 1, c == 0
            to_next = (j, j + 2, LINK["far"])
            to_next_mate = (j + 1, j + 2, LINK["far"] + 1)
            to_last = (j, j - 2, LINK["back"] + 3)
            to_last_mate = (j - 1, j - 2, LINK["back"] + 2)
            own_mate = (j + 1, j, LINK["own"] + 2) if even else (j - 1, j, LINK["own"] + 1)
            places[i * NJ + j] = [
                (up, up - 1, LINK["ahead"] + COLUMN, up > 0),
                (down, down + 1, LINK["behind"] + COLUMN + 1, down + 1 < NI),
                (*to_next, not top),
                (*to_next_mate, even and not top),
                (*to_last, not bottom),
                (*to_last_mate, odd and not bottom),
                (*(to_next if top else to_last), top or bottom),
                (*(to_next_mate if top else to_last_mate), (top and even) or (bottom and odd)),
                (*own_mate, True),
                (i, i, UNIT, True),
                (j, j, UNIT, True),
            ]
    return places


TABLE = tables()


def coefficients(occ_fock, row_links, column_links):
    links = jnp.concatenate([row_links, column_links, jnp.zeros((2,), jnp.int32)])
    got = {
        "own": links,
        "far": send(links, along_j(-2)),
        "back": send(links, along_j(2)),
        "ahead": send(links, GOAL[1]),
        "behind": send(links, GOAL[-1]),
    }
    where = lax.axis_index("ia") * NJ + lax.axis_index("ja")
    place = lax.dynamic_slice_in_dim(jnp.asarray(TABLE), where, 1, axis=0)[0]
    rows, columns, link, used = place[:, 0], place[:, 1], place[:, 2], place[:, 3]
    spots = jnp.arange(NJ, dtype=jnp.int32)
    hot = (rows[:, None, None] == spots[None, :, None]) & (columns[:, None, None] == spots[None, None, :])
    hot = hot & (used[:, None, None] > 0)
    picked = jnp.sum(jnp.where(hot, occ_fock[None], 0.0), axis=(1, 2))
    chosen = link[:, None] == jnp.arange(UNIT + 8, dtype=jnp.int32)[None, :]
    flat = jnp.concatenate([got[name] for name in SOURCES] + [jnp.ones((8,), jnp.int32)])
    weights = jnp.sum(jnp.where(chosen, flat[None, :], 0), axis=1)
    return picked * weights.astype(jnp.float32)


def after(value, earlier):
    return lax.optimization_barrier((value, earlier))[0]


def sweep_pieces(pieces, picked, low):
    at_top = (low == NLO - 1).astype(jnp.float32)
    at_bottom = (low == 0).astype(jnp.float32)
    mates = [send(p, PARTNER) for p in pieces]
    firsts = [{s: send(p, FIRST[s]) for s in (1, -1)} for p in pieces]
    crossed = []
    out = None
    for p, m in zip(pieces, mates):
        if out is not None:
            p = after(p, out)
        out = picked[OUT] * p + picked[OUT_MATE] * m
        crossed.append(send(out, ACROSS))
    middles = []
    up = None
    for f, x in zip(firsts, crossed):
        if up is not None:
            x = after(x, up)
        up = picked[AHEAD] * f[1] + at_bottom * x
        down = picked[BEHIND] * f[-1] + at_top * x
        middles.append({1: send(up, MIDDLE[1]), -1: send(down, MIDDLE[-1])})
    gathered = []
    up = None
    for p, m, mid in zip(pieces, mates, middles):
        if up is not None:
            p = after(p, up)
        up = mid[1] + picked[UP] * p + picked[UP_MATE] * m
        down = mid[-1] + picked[DOWN] * p + picked[DOWN_MATE] * m
        plus = send(up, LAST[1])
        minus = send(down, LAST[-1])
        gathered.append(plus + minus + picked[MATE] * m)
    return gathered


def body(
    amplitudes,
    integrals,
    pao_fock,
    pao_intersection,
    block_columns,
    occ_fock,
    pao_energies,
    row_links,
    column_links,
):
    start = amplitudes[0, 0]
    integral = integrals[0, 0]
    low = (lax.axis_index("ja") // 2) % NLO
    wide = start.shape[0] // CHUNKS
    spans = [slice(k * wide, (k + 1) * wide) for k in range(CHUNKS)]
    pieces = list(lax.optimization_barrier(tuple(start[span] for span in spans)))
    for sweep_number in range(ITERS):
        if sweep_number == 0:
            picked = coefficients(occ_fock, row_links[0, 0], column_links[0, 0])
            diagonal = picked[FIRST_DIAGONAL] + picked[SECOND_DIAGONAL]
            fock_dense = build_dense(pao_fock, block_columns)
            intersection_dense = build_dense(pao_intersection, block_columns)
            shifted = fock_dense - diagonal * intersection_dense
            inverse_gap = 1.0 / (pao_energies[:, None] + pao_energies[None, :] - diagonal)
            current = start
        else:
            current = jnp.concatenate(pieces, axis=0)
        gathered = sweep_pieces(pieces, picked, low)
        from_fock = mm(shifted, current)
        from_intersection = mm(intersection_dense, current)
        local = mm(from_fock, intersection_dense)
        local = local + mm(from_intersection, fock_dense) + integral.astype(jnp.float32)
        rights = [mm(coupled, intersection_dense) for coupled in gathered]
        if sweep_number + 1 == ITERS:
            for right, span in zip(rights, spans):
                local = local - mm(intersection_dense[:, span], right)
            return (current - local * inverse_gap)[None, None]
        rest = [local[span] for span in spans]
        for k, right in enumerate(rights):
            rest = [r - mm(intersection_dense[span, spans[k]], right) for r, span in zip(rest, spans)]
        pieces = [p - r * inverse_gap[span] for p, r, span in zip(pieces, rest, spans)]


def solution(mesh):
    placed = (
        P("ia", "ja", None, None),
        P("ia", "ja", None, None),
        P(),
        P(),
        P(),
        P(),
        P(),
        P("ia", "ja", None),
        P("ia", "ja", None),
    )
    return jax.shard_map(
        body, mesh=mesh, in_specs=placed, out_specs=P("ia", "ja", None, None), check_vma=False
    )
```

```python
import jax
import jax.numpy as jnp
import numpy as np
from jax import lax
from jax.sharding import PartitionSpec as P

ITERS = 2
CHUNKS = 2
NX, NY, NHI, NLO = 4, 4, 4, 4
NZ = NHI * NLO
NI = NY * NHI
NJ = NX * NLO * 2

HIGH = lax.Precision.HIGH
AXES = ("ia", "ja")


def chip(i, j):
    return j // (2 * NLO), i // NHI, (i % NHI) * NLO + (j // 2) % NLO, j % 2


def pair(x, y, z, c):
    z = z % NZ
    return y * NHI + z // NLO, (x * NLO + z % NLO) * 2 + c


def moves(target):
    pairs = []
    for i in range(NI):
        for j in range(NJ):
            to = target(i, j)
            if to is not None:
                pairs.append((i * NJ + j, to[0] * NJ + to[1]))
    return pairs


def first_leg(step):
    def target(i, j):
        if not 0 <= i + step < NI:
            return None
        x, _, z, c = chip(i, j)
        return pair(x, (i + step) // NHI, z + step, c)

    return moves(target)


def middle_leg(step):
    def target(i, j):
        x, y, z, c = chip(i, j)
        di, dj = pair(x, y, z + 3 * step, c)
        edge = NLO - 1 if step > 0 else 0
        if not 0 <= di - step < NI and (dj // 2) % NLO != edge:
            return None
        return pair(x, y, z + 2 * step, c)

    return moves(target)


def last_leg(step):
    def target(i, j):
        x, y, z, c = chip(i, j)
        di, dj = pair(x, y, z + step, c)
        near = 0 if step > 0 else NLO - 1
        if not 0 <= di - step < NI and (dj // 2) % NLO == near:
            return None
        return di, dj

    return moves(target)


def across(i, j):
    x, y, z, c = chip(i, j)
    if z % NLO == NLO - 1 and x + 1 < NX:
        return pair(x + 1, y, z, c)
    if z % NLO == 0 and x > 0:
        return pair(x - 1, y, z, c)
    return None


def goal_links(step):
    def target(i, j):
        x, y, z, c = chip(i, j)
        return pair(x, y, z - 3 * step, c)

    return moves(target)


def along_j(offset):
    def target(i, j):
        return (i, j + offset) if 0 <= j + offset < NJ else None

    return moves(target)


FIRST = {s: first_leg(s) for s in (1, -1)}
MIDDLE = {s: middle_leg(s) for s in (1, -1)}
LAST = {s: last_leg(s) for s in (1, -1)}
ACROSS = moves(across)
PARTNER = moves(lambda i, j: (i, j ^ 1))
GOAL = {s: goal_links(s) for s in (1, -1)}


def send(x, pairs):
    return lax.ppermute(x, AXES, pairs)


def mm(a, b):
    return jnp.dot(a, b, precision=HIGH, preferred_element_type=jnp.float32)


def build_dense(blocks, columns):
    block_rows, block_size, block_wide = blocks.shape
    wide = block_rows * block_size
    slot = jnp.arange(block_wide, dtype=jnp.int32)
    place = jnp.repeat(columns, block_size, axis=1) * block_size + (slot % block_size)[None, :]
    spread = (place[:, :, None] == jnp.arange(wide, dtype=jnp.int32)[None, None, :]).astype(jnp.float32)
    dense = jnp.einsum("rxk,rkn->rxn", blocks, spread, precision=HIGH)
    return dense.reshape(wide, wide)


SOURCES = ("own", "far", "back", "ahead", "behind")
LINK = {name: 8 * n for n, name in enumerate(SOURCES)}
UNIT = 8 * len(SOURCES)
AHEAD, BEHIND, PLUS, PLUS_MATE, MINUS, MINUS_MATE, FIRST_DIAGONAL, SECOND_DIAGONAL = range(8)
UP, UP_MATE, DOWN, DOWN_MATE, OUT, OUT_MATE, MATE = range(7)
COLUMN = 4


def tables():
    places = np.zeros((NI * NJ, 15, 4), np.int32)
    for i in range(NI):
        for j in range(NJ):
            x, y, z, c = chip(i, j)
            low = z % NLO
            up = pair(x, y, z + 3, c)[0]
            down = pair(x, y, z - 3, c)[0]
            top, bottom = low == NLO - 1, low == 0
            odd, even = c == 1, c == 0
            to_next = (j, j + 2, LINK["far"])
            to_next_mate = (j + 1, j + 2, LINK["far"] + 1)
            to_last = (j, j - 2, LINK["back"] + 3)
            to_last_mate = (j - 1, j - 2, LINK["back"] + 2)
            own_mate = (j + 1, j, LINK["own"] + 2) if even else (j - 1, j, LINK["own"] + 1)
            places[i * NJ + j] = [
                (up, up - 1, LINK["ahead"] + COLUMN, up > 0),
                (down, down + 1, LINK["behind"] + COLUMN + 1, down + 1 < NI),
                (j + 8, j + 6, LINK["ahead"] + 3, bottom),
                (j + 7, j + 6, LINK["ahead"] + 2, bottom and odd),
                (j - 8, j - 6, LINK["behind"], top),
                (j - 7, j - 6, LINK["behind"] + 1, top and even),
                (i, i, UNIT, True),
                (j, j, UNIT, True),
                (*to_next, not top),
                (*to_next_mate, even and not top),
                (*to_last, not bottom),
                (*to_last_mate, odd and not bottom),
                (*(to_next if top else to_last), top or bottom),
                (*(to_next_mate if top else to_last_mate), (top and even) or (bottom and odd)),
                (*own_mate, True),
            ]
    places[..., 0] = np.where(places[..., 3] > 0, places[..., 0], -1)
    return places[..., :3].astype(np.int8)


TABLE = tables()


def chosen(place, occ_fock, got):
    rows, columns, link = place[:, 0], place[:, 1], place[:, 2]
    spots = jnp.arange(NJ, dtype=jnp.int32)
    hot = (rows[:, None, None] == spots[None, :, None]) & (columns[:, None, None] == spots[None, None, :])
    picked = jnp.sum(jnp.where(hot, occ_fock[None], 0.0), axis=(1, 2))
    nothing = jnp.zeros((8,), jnp.int32)
    flat = jnp.concatenate([got.get(name, nothing) for name in SOURCES] + [jnp.ones((8,), jnp.int32)])
    taken = link[:, None] == jnp.arange(UNIT + 8, dtype=jnp.int32)[None, :]
    weights = jnp.sum(jnp.where(taken, flat[None, :], 0), axis=1)
    return picked * weights.astype(jnp.float32)


def coefficients(occ_fock, row_links, column_links):
    links = jnp.concatenate([row_links, column_links, jnp.zeros((2,), jnp.int32)])
    where = lax.axis_index("ia") * NJ + lax.axis_index("ja")
    place = lax.dynamic_slice_in_dim(jnp.asarray(TABLE), where, 1, axis=0)[0].astype(jnp.int32)
    first = {"ahead": send(links, GOAL[1]), "behind": send(links, GOAL[-1])}
    rest = {"own": links, "far": send(links, along_j(-2)), "back": send(links, along_j(2))}
    return chosen(place[:8], occ_fock, first), chosen(place[8:], occ_fock, rest)


def after(value, earlier):
    return lax.optimization_barrier((value, earlier))[0]


def sweep_pieces(pieces, first, rest, low, raw):
    at_top = (low == NLO - 1).astype(jnp.float32)
    at_bottom = (low == 0).astype(jnp.float32)
    mates = [send(p, PARTNER) for p in pieces]
    firsts = [{s: send(p, FIRST[s]) for s in (1, -1)} for p in pieces]
    if raw:
        crossed = [send(p, ACROSS) for p in pieces]
        others = [send(x, PARTNER) for x in crossed]
    else:
        crossed = []
        out = None
        for p, m in zip(pieces, mates):
            if out is not None:
                p = after(p, out)
            out = rest[OUT] * p + rest[OUT_MATE] * m
            crossed.append(send(out, ACROSS))
    middles = []
    done = None
    for k, (f, x) in enumerate(zip(firsts, crossed)):
        up, down = f[1], f[-1]
        if done is not None:
            up = after(up, done)
        if raw:
            up = first[AHEAD] * up + first[PLUS] * x + first[PLUS_MATE] * others[k]
            down = first[BEHIND] * after(down, up) + first[MINUS] * x + first[MINUS_MATE] * others[k]
        else:
            up = first[AHEAD] * up + at_bottom * x
            down = first[BEHIND] * after(down, up) + at_top * x
        middles.append({1: send(up, MIDDLE[1]), -1: send(down, MIDDLE[-1])})
        done = down
    gathered = []
    done = None
    for p, m, mid in zip(pieces, mates, middles):
        up, down = mid[1], mid[-1]
        if done is not None:
            up = after(up, done)
        up = up + rest[UP] * p + rest[UP_MATE] * m
        down = after(down, up) + rest[DOWN] * p + rest[DOWN_MATE] * m
        plus = send(up, LAST[1])
        minus = send(down, LAST[-1])
        gathered.append(plus + minus + rest[MATE] * m)
        done = down
    return gathered


def body(
    amplitudes,
    integrals,
    pao_fock,
    pao_intersection,
    block_columns,
    occ_fock,
    pao_energies,
    row_links,
    column_links,
):
    start = amplitudes[0, 0]
    integral = integrals[0, 0]
    low = (lax.axis_index("ja") // 2) % NLO
    wide = start.shape[0] // CHUNKS
    spans = [slice(k * wide, (k + 1) * wide) for k in range(CHUNKS)]
    pieces = list(lax.optimization_barrier(tuple(start[span] for span in spans)))
    for sweep_number in range(ITERS):
        if sweep_number == 0:
            first, rest = coefficients(occ_fock, row_links[0, 0], column_links[0, 0])
            diagonal = first[FIRST_DIAGONAL] + first[SECOND_DIAGONAL]
            fock_dense = build_dense(pao_fock, block_columns)
            intersection_dense = build_dense(pao_intersection, block_columns)
            shifted = fock_dense - diagonal * intersection_dense
            inverse_gap = 1.0 / (pao_energies[:, None] + pao_energies[None, :] - diagonal)
            current = start
        else:
            current = jnp.concatenate(pieces, axis=0)
        gathered = sweep_pieces(pieces, first, rest, low, sweep_number == 0)
        from_fock = mm(shifted, current)
        from_intersection = mm(intersection_dense, current)
        local = mm(from_fock, intersection_dense)
        local = local + mm(from_intersection, fock_dense) + integral.astype(jnp.float32)
        rights = [mm(coupled, intersection_dense) for coupled in gathered]
        if sweep_number + 1 == ITERS:
            for right, span in zip(rights, spans):
                local = local - mm(intersection_dense[:, span], right)
            return (current - local * inverse_gap)[None, None]
        parts = [local[span] for span in spans]
        for k, right in enumerate(rights):
            parts = [r - mm(intersection_dense[span, spans[k]], right) for r, span in zip(parts, spans)]
        pieces = [p - r * inverse_gap[span] for p, r, span in zip(pieces, parts, spans)]


def solution(mesh):
    placed = (
        P("ia", "ja", None, None),
        P("ia", "ja", None, None),
        P(),
        P(),
        P(),
        P(),
        P(),
        P("ia", "ja", None),
        P("ia", "ja", None),
    )
    return jax.shard_map(
        body, mesh=mesh, in_specs=placed, out_specs=P("ia", "ja", None, None), check_vma=False
    )
```

```python
import jax
import jax.numpy as jnp
import numpy as np
from jax import lax
from jax.sharding import PartitionSpec as P

ITERS = 2
CHUNKS = 2
NX, NY, NHI, NLO = 4, 4, 4, 4
NZ = NHI * NLO
NI = NY * NHI
NJ = NX * NLO * 2

HIGH = lax.Precision.HIGH
AXES = ("ia", "ja")


def chip(i, j):
    return j // (2 * NLO), i // NHI, (i % NHI) * NLO + (j // 2) % NLO, j % 2


def pair(x, y, z, c):
    z = z % NZ
    return y * NHI + z // NLO, (x * NLO + z % NLO) * 2 + c


def moves(target):
    pairs = []
    for i in range(NI):
        for j in range(NJ):
            to = target(i, j)
            if to is not None:
                pairs.append((i * NJ + j, to[0] * NJ + to[1]))
    return pairs


def first_leg(step):
    def target(i, j):
        if not 0 <= i + step < NI:
            return None
        x, _, z, c = chip(i, j)
        return pair(x, (i + step) // NHI, z + step, c)

    return moves(target)


def middle_leg(step):
    def target(i, j):
        x, y, z, c = chip(i, j)
        di, dj = pair(x, y, z + 3 * step, c)
        edge = NLO - 1 if step > 0 else 0
        if not 0 <= di - step < NI and (dj // 2) % NLO != edge:
            return None
        return pair(x, y, z + 2 * step, c)

    return moves(target)


def last_leg(step):
    def target(i, j):
        x, y, z, c = chip(i, j)
        di, dj = pair(x, y, z + step, c)
        near = 0 if step > 0 else NLO - 1
        if not 0 <= di - step < NI and (dj // 2) % NLO == near:
            return None
        return di, dj

    return moves(target)


def across(i, j):
    x, y, z, c = chip(i, j)
    if z % NLO == NLO - 1 and x + 1 < NX:
        return pair(x + 1, y, z, c)
    if z % NLO == 0 and x > 0:
        return pair(x - 1, y, z, c)
    return None


def goal_links(step):
    def target(i, j):
        x, y, z, c = chip(i, j)
        return pair(x, y, z - 3 * step, c)

    return moves(target)


def along_j(offset):
    def target(i, j):
        return (i, j + offset) if 0 <= j + offset < NJ else None

    return moves(target)


FIRST = {s: first_leg(s) for s in (1, -1)}
MIDDLE = {s: middle_leg(s) for s in (1, -1)}
LAST = {s: last_leg(s) for s in (1, -1)}
ACROSS = moves(across)
PARTNER = moves(lambda i, j: (i, j ^ 1))
GOAL = {s: goal_links(s) for s in (1, -1)}


def send(x, pairs):
    return lax.ppermute(x, AXES, pairs)


def mm(a, b):
    return jnp.dot(a, b, precision=HIGH, preferred_element_type=jnp.float32)


def build_dense(blocks, columns):
    block_rows, block_size, block_wide = blocks.shape
    wide = block_rows * block_size
    slot = jnp.arange(block_wide, dtype=jnp.int32)
    place = jnp.repeat(columns, block_size, axis=1) * block_size + (slot % block_size)[None, :]
    spread = (place[:, :, None] == jnp.arange(wide, dtype=jnp.int32)[None, None, :]).astype(jnp.float32)
    dense = jnp.einsum("rxk,rkn->rxn", blocks, spread, precision=HIGH)
    return dense.reshape(wide, wide)


SOURCES = ("own", "far", "back", "ahead", "behind")
LINK = {name: 8 * n for n, name in enumerate(SOURCES)}
UNIT = 8 * len(SOURCES)
AHEAD, BEHIND, PLUS, PLUS_MATE, MINUS, MINUS_MATE, FIRST_DIAGONAL, SECOND_DIAGONAL = range(8)
UP, UP_MATE, DOWN, DOWN_MATE, OUT, OUT_MATE, MATE = range(7)
COLUMN = 4


def tables():
    places = np.zeros((NI * NJ, 15, 4), np.int32)
    for i in range(NI):
        for j in range(NJ):
            x, y, z, c = chip(i, j)
            low = z % NLO
            up = pair(x, y, z + 3, c)[0]
            down = pair(x, y, z - 3, c)[0]
            top, bottom = low == NLO - 1, low == 0
            odd, even = c == 1, c == 0
            to_next = (j, j + 2, LINK["far"])
            to_next_mate = (j + 1, j + 2, LINK["far"] + 1)
            to_last = (j, j - 2, LINK["back"] + 3)
            to_last_mate = (j - 1, j - 2, LINK["back"] + 2)
            own_mate = (j + 1, j, LINK["own"] + 2) if even else (j - 1, j, LINK["own"] + 1)
            places[i * NJ + j] = [
                (up, up - 1, LINK["ahead"] + COLUMN, up > 0),
                (down, down + 1, LINK["behind"] + COLUMN + 1, down + 1 < NI),
                (j + 8, j + 6, LINK["ahead"] + 3, bottom),
                (j + 7, j + 6, LINK["ahead"] + 2, bottom and odd),
                (j - 8, j - 6, LINK["behind"], top),
                (j - 7, j - 6, LINK["behind"] + 1, top and even),
                (i, i, UNIT, True),
                (j, j, UNIT, True),
                (*to_next, not top),
                (*to_next_mate, even and not top),
                (*to_last, not bottom),
                (*to_last_mate, odd and not bottom),
                (*(to_next if top else to_last), top or bottom),
                (*(to_next_mate if top else to_last_mate), (top and even) or (bottom and odd)),
                (*own_mate, True),
            ]
    places[..., 0] = np.where(places[..., 3] > 0, places[..., 0], -1)
    return places[..., :3].astype(np.int8)


TABLE = tables()


def chosen(place, occ_fock, got):
    rows, columns, link = place[:, 0], place[:, 1], place[:, 2]
    spots = jnp.arange(NJ, dtype=jnp.int32)
    hot = (rows[:, None, None] == spots[None, :, None]) & (columns[:, None, None] == spots[None, None, :])
    picked = jnp.sum(jnp.where(hot, occ_fock[None], 0.0), axis=(1, 2))
    nothing = jnp.zeros((8,), jnp.int32)
    flat = jnp.concatenate([got.get(name, nothing) for name in SOURCES] + [jnp.ones((8,), jnp.int32)])
    taken = link[:, None] == jnp.arange(UNIT + 8, dtype=jnp.int32)[None, :]
    weights = jnp.sum(jnp.where(taken, flat[None, :], 0), axis=1)
    return picked * weights.astype(jnp.float32)


def coefficients(occ_fock, row_links, column_links):
    links = jnp.concatenate([row_links, column_links, jnp.zeros((2,), jnp.int32)])
    where = lax.axis_index("ia") * NJ + lax.axis_index("ja")
    place = lax.dynamic_slice_in_dim(jnp.asarray(TABLE), where, 1, axis=0)[0].astype(jnp.int32)
    first = {"ahead": send(links, GOAL[1]), "behind": send(links, GOAL[-1])}
    rest = {"own": links, "far": send(links, along_j(-2)), "back": send(links, along_j(2))}
    return chosen(place[:8], occ_fock, first), chosen(place[8:], occ_fock, rest)


def after(value, earlier):
    return lax.optimization_barrier((value, earlier))[0]


def sweep_pieces(pieces, first, rest, low, raw):
    at_top = (low == NLO - 1).astype(jnp.float32)
    at_bottom = (low == 0).astype(jnp.float32)
    mates = [send(p, PARTNER) for p in pieces]
    firsts = [{s: send(p, FIRST[s]) for s in (1, -1)} for p in pieces]
    if raw:
        crossed = [send(p, ACROSS) for p in pieces]
        others = [send(x, PARTNER) for x in crossed]
    else:
        crossed = []
        out = None
        for p, m in zip(pieces, mates):
            if out is not None:
                p = after(p, out)
            out = rest[OUT] * p + rest[OUT_MATE] * m
            crossed.append(send(out, ACROSS))
    middles = []
    done = None
    for k, (f, x) in enumerate(zip(firsts, crossed)):
        if done is not None:
            x = after(x, done)
        if raw:
            up = first[AHEAD] * f[1] + first[PLUS] * x + first[PLUS_MATE] * others[k]
            down = first[BEHIND] * f[-1] + first[MINUS] * x + first[MINUS_MATE] * others[k]
        else:
            up = first[AHEAD] * f[1] + at_bottom * x
            down = first[BEHIND] * f[-1] + at_top * x
        middles.append({1: send(up, MIDDLE[1]), -1: send(down, MIDDLE[-1])})
        done = up
    near = [
        {1: rest[UP] * p + rest[UP_MATE] * m, -1: rest[DOWN] * p + rest[DOWN_MATE] * m}
        for p, m in zip([after(p, done) for p in pieces], mates)
    ]
    near = lax.optimization_barrier(near)
    gathered = []
    for m, mid, add in zip(mates, middles, near):
        plus = send(mid[1] + add[1], LAST[1])
        minus = send(mid[-1] + add[-1], LAST[-1])
        gathered.append(plus + minus + rest[MATE] * m)
    return gathered


def body(
    amplitudes,
    integrals,
    pao_fock,
    pao_intersection,
    block_columns,
    occ_fock,
    pao_energies,
    row_links,
    column_links,
):
    start = amplitudes[0, 0]
    integral = integrals[0, 0]
    low = (lax.axis_index("ja") // 2) % NLO
    wide = start.shape[0] // CHUNKS
    spans = [slice(k * wide, (k + 1) * wide) for k in range(CHUNKS)]
    pieces = list(lax.optimization_barrier(tuple(start[span] for span in spans)))
    for sweep_number in range(ITERS):
        if sweep_number == 0:
            first, rest = coefficients(occ_fock, row_links[0, 0], column_links[0, 0])
            diagonal = first[FIRST_DIAGONAL] + first[SECOND_DIAGONAL]
            fock_dense = build_dense(pao_fock, block_columns)
            intersection_dense = build_dense(pao_intersection, block_columns)
            shifted = fock_dense - diagonal * intersection_dense
            inverse_gap = 1.0 / (pao_energies[:, None] + pao_energies[None, :] - diagonal)
            current = start
        else:
            current = jnp.concatenate(pieces, axis=0)
        gathered = sweep_pieces(pieces, first, rest, low, sweep_number == 0)
        from_fock = mm(shifted, current)
        from_intersection = mm(intersection_dense, current)
        local = mm(from_fock, intersection_dense)
        local = local + mm(from_intersection, fock_dense) + integral.astype(jnp.float32)
        rights = [mm(coupled, intersection_dense) for coupled in gathered]
        if sweep_number + 1 == ITERS:
            for right, span in zip(rights, spans):
                local = local - mm(intersection_dense[:, span], right)
            return (current - local * inverse_gap)[None, None]
        parts = [local[span] for span in spans]
        for k, right in enumerate(rights):
            parts = [r - mm(intersection_dense[span, spans[k]], right) for r, span in zip(parts, spans)]
        pieces = [p - r * inverse_gap[span] for p, r, span in zip(pieces, parts, spans)]


def solution(mesh):
    placed = (
        P("ia", "ja", None, None),
        P("ia", "ja", None, None),
        P(),
        P(),
        P(),
        P(),
        P(),
        P("ia", "ja", None),
        P("ia", "ja", None),
    )
    return jax.shard_map(
        body, mesh=mesh, in_specs=placed, out_specs=P("ia", "ja", None, None), check_vma=False
    )
```

```python
import jax
import jax.numpy as jnp
import numpy as np
from jax import lax
from jax.sharding import PartitionSpec as P

ITERS = 2
NX, NY, NHI, NLO = 4, 4, 4, 4
NZ = NHI * NLO
NI = NY * NHI
NJ = NX * NLO * 2

HIGH = lax.Precision.HIGH
AXES = ("ia", "ja")


def chip(i, j):
    return j // (2 * NLO), i // NHI, (i % NHI) * NLO + (j // 2) % NLO, j % 2


def pair(x, y, z, c):
    z = z % NZ
    return y * NHI + z // NLO, (x * NLO + z % NLO) * 2 + c


def moves(target):
    pairs = []
    for i in range(NI):
        for j in range(NJ):
            to = target(i, j)
            if to is not None:
                pairs.append((i * NJ + j, to[0] * NJ + to[1]))
    return pairs


def way(core):
    return 1 - 2 * core


def first_leg(mate):
    def target(i, j):
        x, _, z, c = chip(i, j)
        relay = 1 - c if mate else c
        step = way(relay)
        if not 0 <= i + step < NI:
            return None
        return pair(x, (i + step) // NHI, z + step, relay)

    return moves(target)


def middle_leg(i, j):
    x, y, z, c = chip(i, j)
    step = way(c)
    di, dj = pair(x, y, z + 3 * step, c)
    edge = NLO - 1 if step > 0 else 0
    if not 0 <= di - step < NI and (dj // 2) % NLO != edge:
        return None
    return pair(x, y, z + 2 * step, c)


def last_leg(mate):
    def target(i, j):
        x, y, z, c = chip(i, j)
        step = way(c)
        di, dj = pair(x, y, z + step, 1 - c if mate else c)
        near = 0 if step > 0 else NLO - 1
        if not 0 <= di - step < NI and (dj // 2) % NLO == near:
            return None
        return di, dj

    return moves(target)


def across(mate):
    def target(i, j):
        x, y, z, c = chip(i, j)
        relay = 1 - c if mate else c
        if z % NLO == 0 and relay == 0 and x > 0:
            return pair(x - 1, y, z, relay)
        if z % NLO == NLO - 1 and relay == 1 and x + 1 < NX:
            return pair(x + 1, y, z, relay)
        return None

    return moves(target)


def goal_links(hops, mate):
    def target(i, j):
        x, y, z, c = chip(i, j)
        relay = 1 - c if mate else c
        return pair(x, y, z - hops * way(relay), relay)

    return moves(target)


FIRST = {"A": first_leg(False), "B": first_leg(True)}
MIDDLE = moves(middle_leg)
LAST = {"A": last_leg(False), "B": last_leg(True)}
ACROSS = {"A": across(False), "B": across(True)}
PARTNER = moves(lambda i, j: (i, j ^ 1))


def send(x, pairs):
    return lax.ppermute(x, AXES, pairs)


def mm(a, b):
    return jnp.dot(a, b, precision=HIGH, preferred_element_type=jnp.float32)


def build_dense(blocks, columns):
    block_rows, block_size, block_wide = blocks.shape
    wide = block_rows * block_size
    slot = jnp.arange(block_wide, dtype=jnp.int32)
    place = jnp.repeat(columns, block_size, axis=1) * block_size + (slot % block_size)[None, :]
    spread = (place[:, :, None] == jnp.arange(wide, dtype=jnp.int32)[None, None, :]).astype(jnp.float32)
    dense = jnp.einsum("rxk,rkn->rxn", blocks, spread, precision=HIGH)
    return dense.reshape(wide, wide)


SOURCES = ("own", "far", "far_mate", "next", "next_mate")
LINK = {name: 8 * n for n, name in enumerate(SOURCES)}
UNIT = 8 * len(SOURCES)
(
    PASS,
    PASS_MATE,
    CROSS,
    CROSS_MATE,
    CROSS_OWN,
    NEAR,
    NEAR_OTHER,
    NEAR_MATE,
    MATE,
    FIRST_DIAGONAL,
    SECOND_DIAGONAL,
) = range(11)
COLUMN = 4


def tables():
    places = np.zeros((NI * NJ, 11, 3), np.int8)
    for i in range(NI):
        for j in range(NJ):
            x, y, z, c = chip(i, j)
            s = way(c)
            low = z % NLO
            di, dj = pair(x, y, z + 3 * s, c)
            _, nj = pair(x, y, z + s, c)
            inside = 0 <= di - s < NI
            crosses = low == (0 if s > 0 else NLO - 1)
            joins = low != (NLO - 1 if s > 0 else 0)
            column = COLUMN + (0 if s > 0 else 1)
            on2, on1, back2, back1 = (3, 2, 0, 1) if s > 0 else (0, 1, 3, 2)
            entries = [
                (di, di - s, LINK["far"] + column, inside),
                (di, di - s, LINK["far_mate"] + column, inside),
                (dj + 2 * s, dj, LINK["far"] + on2, crosses),
                (dj + 3 * s, dj + s, LINK["far_mate"] + on2, crosses),
                (dj + 2 * s, dj + s, LINK["far_mate"] + on1, crosses),
                (j, nj, LINK["next"] + back2, joins),
                (j + s, nj, LINK["next"] + back1, joins),
                (j + s, nj + s, LINK["next_mate"] + back2, joins),
                (j + s, j, LINK["own"] + on1, True),
                (i, i, UNIT, True),
                (j, j, UNIT, True),
            ]
            for n, (row, to, link, used) in enumerate(entries):
                used = used and 0 <= row < NJ and 0 <= to < NJ
                places[i * NJ + j, n] = (row, to, link) if used else (-1, 0, 0)
    return places


TABLE = tables()


def chosen(place, occ_fock, got):
    rows, columns, link = place[:, 0], place[:, 1], place[:, 2]
    spots = jnp.arange(NJ, dtype=jnp.int32)
    hot = (rows[:, None, None] == spots[None, :, None]) & (columns[:, None, None] == spots[None, None, :])
    picked = jnp.sum(jnp.where(hot, occ_fock[None], 0.0), axis=(1, 2))
    nothing = jnp.zeros((8,), jnp.int32)
    flat = jnp.concatenate([got.get(name, nothing) for name in SOURCES] + [jnp.ones((8,), jnp.int32)])
    taken = link[:, None] == jnp.arange(UNIT + 8, dtype=jnp.int32)[None, :]
    weights = jnp.sum(jnp.where(taken, flat[None, :], 0), axis=1)
    return picked * weights.astype(jnp.float32)


def coefficients(occ_fock, row_links, column_links):
    links = jnp.concatenate([row_links, column_links, jnp.zeros((2,), jnp.int32)])
    where = lax.axis_index("ia") * NJ + lax.axis_index("ja")
    place = lax.dynamic_slice_in_dim(jnp.asarray(TABLE), where, 1, axis=0)[0].astype(jnp.int32)
    got = {
        "own": links,
        "far": send(links, goal_links(3, False)),
        "far_mate": send(links, goal_links(3, True)),
        "next": send(links, goal_links(1, False)),
        "next_mate": send(links, goal_links(1, True)),
    }
    return chosen(place, occ_fock, got)


def after(value, earlier):
    return lax.optimization_barrier((value, earlier))[0]


def neighbour_sum(current, weight):
    cross_own = send(current, ACROSS["A"])
    first_own = send(current, FIRST["A"])
    mate = send(current, PARTNER)
    cross_mate = send(current, ACROSS["B"])
    first_mate = send(current, FIRST["B"])
    passed = weight[PASS] * first_own + weight[CROSS] * cross_own
    middle_own = send(passed, MIDDLE)
    cross_own = after(cross_own, passed)
    passed = weight[PASS_MATE] * first_mate + weight[CROSS_MATE] * cross_mate + weight[CROSS_OWN] * cross_own
    middle_mate = send(passed, MIDDLE)
    held = after(current, passed)
    near = (weight[NEAR] * held + weight[NEAR_OTHER] * mate, weight[NEAR_MATE] * mate)
    near_own, near_mate = lax.optimization_barrier(near)
    last_own = send(middle_own + near_own, LAST["A"])
    last_mate = send(middle_mate + near_mate, LAST["B"])
    return last_own + weight[MATE] * mate, last_mate


def body(
    amplitudes,
    integrals,
    pao_fock,
    pao_intersection,
    block_columns,
    occ_fock,
    pao_energies,
    row_links,
    column_links,
):
    start = amplitudes[0, 0]
    integral = integrals[0, 0]
    current = start
    for sweep_number in range(ITERS):
        if sweep_number == 0:
            weight = coefficients(occ_fock, row_links[0, 0], column_links[0, 0])
            diagonal = weight[FIRST_DIAGONAL] + weight[SECOND_DIAGONAL]
            fock_dense = build_dense(pao_fock, block_columns)
            intersection_dense = build_dense(pao_intersection, block_columns)
            shifted = fock_dense - diagonal * intersection_dense
            inverse_gap = 1.0 / (pao_energies[:, None] + pao_energies[None, :] - diagonal)
        parts = neighbour_sum(current, weight)
        from_fock = mm(shifted, current)
        from_intersection = mm(intersection_dense, current)
        local = mm(from_fock, intersection_dense)
        local = local + mm(from_intersection, fock_dense) + integral.astype(jnp.float32)
        for part in parts:
            local = local - mm(intersection_dense, mm(part, intersection_dense))
        current = current - local * inverse_gap
    return current[None, None]


def solution(mesh):
    placed = (
        P("ia", "ja", None, None),
        P("ia", "ja", None, None),
        P(),
        P(),
        P(),
        P(),
        P(),
        P("ia", "ja", None),
        P("ia", "ja", None),
    )
    return jax.shard_map(
        body, mesh=mesh, in_specs=placed, out_specs=P("ia", "ja", None, None), check_vma=False
    )
```

```python
import jax
import jax.numpy as jnp
import numpy as np
from jax import lax
from jax.sharding import PartitionSpec as P

ITERS = 2
NX, NY, NHI, NLO = 4, 4, 4, 4
NZ = NHI * NLO
NI = NY * NHI
NJ = NX * NLO * 2

HIGH = lax.Precision.HIGH
AXES = ("ia", "ja")


def chip(i, j):
    return j // (2 * NLO), i // NHI, (i % NHI) * NLO + (j // 2) % NLO, j % 2


def pair(x, y, z, c):
    z = z % NZ
    return y * NHI + z // NLO, (x * NLO + z % NLO) * 2 + c


def moves(target):
    pairs = []
    for i in range(NI):
        for j in range(NJ):
            to = target(i, j)
            if to is not None:
                pairs.append((i * NJ + j, to[0] * NJ + to[1]))
    return pairs


def way(core):
    return 1 - 2 * core


def first_leg(mate):
    def target(i, j):
        x, _, z, c = chip(i, j)
        relay = 1 - c if mate else c
        step = way(relay)
        if not 0 <= i + step < NI:
            return None
        return pair(x, (i + step) // NHI, z + step, relay)

    return moves(target)


def middle_leg(i, j):
    x, y, z, c = chip(i, j)
    step = way(c)
    di, dj = pair(x, y, z + 3 * step, c)
    edge = NLO - 1 if step > 0 else 0
    if not 0 <= di - step < NI and (dj // 2) % NLO != edge:
        return None
    return pair(x, y, z + 2 * step, c)


def last_leg(mate):
    def target(i, j):
        x, y, z, c = chip(i, j)
        step = way(c)
        di, dj = pair(x, y, z + step, 1 - c if mate else c)
        near = 0 if step > 0 else NLO - 1
        if not 0 <= di - step < NI and (dj // 2) % NLO == near:
            return None
        return di, dj

    return moves(target)


def across(mate):
    def target(i, j):
        x, y, z, c = chip(i, j)
        relay = 1 - c if mate else c
        if z % NLO == 0 and relay == 0 and x > 0:
            return pair(x - 1, y, z, relay)
        if z % NLO == NLO - 1 and relay == 1 and x + 1 < NX:
            return pair(x + 1, y, z, relay)
        return None

    return moves(target)


def goal_links(hops, mate):
    def target(i, j):
        x, y, z, c = chip(i, j)
        relay = 1 - c if mate else c
        return pair(x, y, z - hops * way(relay), relay)

    return moves(target)


FIRST = {"A": first_leg(False), "B": first_leg(True)}
MIDDLE = moves(middle_leg)
LAST = {"A": last_leg(False), "B": last_leg(True)}
ACROSS = {"A": across(False), "B": across(True)}
PARTNER = moves(lambda i, j: (i, j ^ 1))


def send(x, pairs):
    return lax.ppermute(x, AXES, pairs)


def mm(a, b):
    return jnp.dot(a, b, precision=HIGH, preferred_element_type=jnp.float32)


def build_dense(blocks, columns):
    block_rows, block_size, block_wide = blocks.shape
    wide = block_rows * block_size
    slot = jnp.arange(block_wide, dtype=jnp.int32)
    place = jnp.repeat(columns, block_size, axis=1) * block_size + (slot % block_size)[None, :]
    spread = (place[:, :, None] == jnp.arange(wide, dtype=jnp.int32)[None, None, :]).astype(jnp.float32)
    dense = jnp.einsum("rxk,rkn->rxn", blocks, spread, precision=HIGH)
    return dense.reshape(wide, wide)


SOURCES = ("own", "far", "far_mate", "next", "next_mate")
LINK = {name: 8 * n for n, name in enumerate(SOURCES)}
UNIT = 8 * len(SOURCES)
PASS, PASS_MATE, CROSS, CROSS_MATE, CROSS_OWN, FIRST_DIAGONAL, SECOND_DIAGONAL = range(7)
NEAR, NEAR_OTHER, NEAR_MATE, MATE = range(4)
COLUMN = 4


def tables():
    places = np.zeros((NI * NJ, 11, 3), np.int8)
    for i in range(NI):
        for j in range(NJ):
            x, y, z, c = chip(i, j)
            s = way(c)
            low = z % NLO
            di, dj = pair(x, y, z + 3 * s, c)
            _, nj = pair(x, y, z + s, c)
            inside = 0 <= di - s < NI
            crosses = low == (0 if s > 0 else NLO - 1)
            joins = low != (NLO - 1 if s > 0 else 0)
            column = COLUMN + (0 if s > 0 else 1)
            on2, on1, back2, back1 = (3, 2, 0, 1) if s > 0 else (0, 1, 3, 2)
            entries = [
                (di, di - s, LINK["far"] + column, inside),
                (di, di - s, LINK["far_mate"] + column, inside),
                (dj + 2 * s, dj, LINK["far"] + on2, crosses),
                (dj + 3 * s, dj + s, LINK["far_mate"] + on2, crosses),
                (dj + 2 * s, dj + s, LINK["far_mate"] + on1, crosses),
                (i, i, UNIT, True),
                (j, j, UNIT, True),
                (j, nj, LINK["next"] + back2, joins),
                (j + s, nj, LINK["next"] + back1, joins),
                (j + s, nj + s, LINK["next_mate"] + back2, joins),
                (j + s, j, LINK["own"] + on1, True),
            ]
            for n, (row, to, link, used) in enumerate(entries):
                used = used and 0 <= row < NJ and 0 <= to < NJ
                places[i * NJ + j, n] = (row, to, link) if used else (-1, 0, 0)
    return places


TABLE = tables()


def chosen(place, occ_fock, got):
    rows, columns, link = place[:, 0], place[:, 1], place[:, 2]
    spots = jnp.arange(NJ, dtype=jnp.int32)
    hot = (rows[:, None, None] == spots[None, :, None]) & (columns[:, None, None] == spots[None, None, :])
    picked = jnp.sum(jnp.where(hot, occ_fock[None], 0.0), axis=(1, 2))
    nothing = jnp.zeros((8,), jnp.int32)
    flat = jnp.concatenate([got.get(name, nothing) for name in SOURCES] + [jnp.ones((8,), jnp.int32)])
    taken = link[:, None] == jnp.arange(UNIT + 8, dtype=jnp.int32)[None, :]
    weights = jnp.sum(jnp.where(taken, flat[None, :], 0), axis=1)
    return picked * weights.astype(jnp.float32)


def coefficients(occ_fock, row_links, column_links):
    links = jnp.concatenate([row_links, column_links, jnp.zeros((2,), jnp.int32)])
    where = lax.axis_index("ia") * NJ + lax.axis_index("ja")
    place = lax.dynamic_slice_in_dim(jnp.asarray(TABLE), where, 1, axis=0)[0].astype(jnp.int32)
    far = {"far": send(links, goal_links(3, False)), "far_mate": send(links, goal_links(3, True))}
    close = {"own": links, "next": send(links, goal_links(1, False)), "next_mate": send(links, goal_links(1, True))}
    first = chosen(place[:7], occ_fock, far)
    return first, chosen(place[7:], occ_fock, close)


def after(value, earlier):
    return lax.optimization_barrier((value, earlier))[0]


def neighbour_sum(current, weight, last_weight):
    cross_own = send(current, ACROSS["A"])
    first_own = send(current, FIRST["A"])
    mate = send(current, PARTNER)
    cross_mate = send(current, ACROSS["B"])
    first_mate = send(current, FIRST["B"])
    passed = weight[PASS] * first_own + weight[CROSS] * cross_own
    middle_own = send(passed, MIDDLE)
    cross_own = after(cross_own, passed)
    passed = weight[PASS_MATE] * first_mate + weight[CROSS_MATE] * cross_mate + weight[CROSS_OWN] * cross_own
    middle_mate = send(passed, MIDDLE)
    held = after(current, passed)
    near = (last_weight[NEAR] * held + last_weight[NEAR_OTHER] * mate, last_weight[NEAR_MATE] * mate)
    near_own, near_mate = lax.optimization_barrier(near)
    last_own = send(middle_own + near_own, LAST["A"])
    last_mate = send(middle_mate + near_mate, LAST["B"])
    return last_own + last_weight[MATE] * mate, last_mate


def body(
    amplitudes,
    integrals,
    pao_fock,
    pao_intersection,
    block_columns,
    occ_fock,
    pao_energies,
    row_links,
    column_links,
):
    start = amplitudes[0, 0]
    integral = integrals[0, 0]
    current = start
    for sweep_number in range(ITERS):
        if sweep_number == 0:
            weight, last_weight = coefficients(occ_fock, row_links[0, 0], column_links[0, 0])
            diagonal = weight[FIRST_DIAGONAL] + weight[SECOND_DIAGONAL]
            fock_dense = build_dense(pao_fock, block_columns)
            intersection_dense = build_dense(pao_intersection, block_columns)
            shifted = fock_dense - diagonal * intersection_dense
            inverse_gap = 1.0 / (pao_energies[:, None] + pao_energies[None, :] - diagonal)
        parts = neighbour_sum(current, weight, last_weight)
        from_fock = mm(shifted, current)
        from_intersection = mm(intersection_dense, current)
        local = mm(from_fock, intersection_dense)
        local = local + mm(from_intersection, fock_dense) + integral.astype(jnp.float32)
        for part in parts:
            local = local - mm(intersection_dense, mm(part, intersection_dense))
        current = current - local * inverse_gap
    return current[None, None]


def solution(mesh):
    placed = (
        P("ia", "ja", None, None),
        P("ia", "ja", None, None),
        P(),
        P(),
        P(),
        P(),
        P(),
        P("ia", "ja", None),
        P("ia", "ja", None),
    )
    return jax.shard_map(
        body, mesh=mesh, in_specs=placed, out_specs=P("ia", "ja", None, None), check_vma=False
    )
```
